32 devices in a mesh: group: 2 (over y), replica: 16 (over z, x, core).
Axes of the slice: x: 2, y: 2, z: 4, core: 2. Of those that a mesh axis runs over, the one named last changes fastest.
Arguments:
- tokens: bfloat16 [32, 144, 896], P(('group', 'replica')), may hold values from -6 to 6
- segments: int32 [32, 144], P(('group', 'replica')), may hold values from 0 to 35, never falling along the last dimension, each value on 1 to 72 neighbouring positions
- norm1_gain: bfloat16 [896], P('group'), may hold values from 0.5 to 1.5
- qkv_weight: bfloat16 [896, 1152], P('group'), may hold values from -0.1875 to 0.1875
- qkv_bias: bfloat16 [1152], P('group'), may hold values from -2.5 to 2.5
- out_weight: bfloat16 [896, 896], P('group'), may hold values from -0.375 to 0.375
- norm2_gain: bfloat16 [896], P('group'), may hold values from 0.5 to 1.5
- gate_weight: bfloat16 [896, 4864], P(None, 'group'), may hold values from -0.1875 to 0.1875
- up_weight: bfloat16 [896, 4864], P(None, 'group'), may hold values from -0.1875 to 0.1875
- down_weight: bfloat16 [4864, 896], P('group'), may hold values from -0.078125 to 0.078125
- cotangent: bfloat16 [32, 144, 896], P(('group', 'replica')), may hold values from -6 to 6
Outputs:
- result: float32 [32, 144, 896], P(('group', 'replica'))
- back_tokens: float32 [32, 144, 896], P(('group', 'replica'))
- grad_norm1: float32 [896], P('group')
- grad_qkv: float32 [896, 1152], P('group')
- grad_bias: float32 [1152], P('group')
- grad_out: float32 [896, 896], P('group')
- grad_norm2: float32 [896], P('group')
- grad_gate: float32 [896, 4864], P(None, 'group')
- grad_up: float32 [896, 4864], P(None, 'group')
- grad_down: float32 [4864, 896], P('group')
The draws below stay inside these ranges and needn't reach their ends.
Inputs may be any that keep to these rules, and one draw needn't show every extreme that they name: `segments`: segment ids never fall along a sequence.
All inputs are finite; a program needn't handle non-finite values.
Results may differ from the reference program's by a relative error of at most 0.023.
Values may be sent and summed in bfloat16 or wider, within the bound.
A program may use at most 192 MiB of HBM per device.

```python
import math
import jax
import jax.numpy as jnp
import numpy as np
from jax import lax

D = 896
H = 14
KV = 2
HD = 64
FF = 4864
SEQ = 144
QKV = 1152
HQ = 896
SEQS = 32


def draw_qkv_bias(key, part):
    key_base = jax.random.fold_in(key, 17)
    values = 0.5 * jax.random.normal(key_base, (QKV,), jnp.float32)
    return jnp.clip(values, -2.5, 2.5).astype(jnp.bfloat16)


def block_levels(stream_key, extent, cuts, least, top_value):
    loudness = 1.0
    for axis_at, shards_of in cuts:
        draws = jax.random.uniform(jax.random.fold_in(jax.random.fold_in(stream_key, 6), axis_at), (shards_of,), jnp.float32, least / len(cuts), top_value / len(cuts))
        loudness = loudness * jnp.repeat(jnp.exp(draws), extent[axis_at] // shards_of).reshape((-1,) + (1,) * (len(extent) - 1 - axis_at))
    return loudness


def split_up(number_of, total, limit, lean):
    weights = [(1 << 20) // math.isqrt(rank ** lean) + 1 for rank in range(2, number_of + 1)]
    spare, holding = total - limit - (number_of - 1), [1] * (number_of - 1)
    while spare > 0:
        free = [i for i in range(number_of - 1) if holding[i] < limit]
        pool, left = sum([weights[i] for i in free]), spare
        for i in free:
            addition = min(limit - holding[i], max(1, left * weights[i] // pool), spare)
            holding[i] = holding[i] + addition
            spare = spare - addition
    return np.array([limit] + holding)


def uneven(key, number_of, total, reach, slope):
    if number_of == 2:
        one = jax.random.randint(key, (), max(1, total - reach), min(reach, total - 1) + 1)
        return jnp.stack([one, total - one])
    tallies = jnp.asarray(split_up(number_of, total, reach, slope), jnp.int32)
    twos = (number_of - 1) // 2
    donor, receiver = tallies[1:1 + 2 * twos:2], tallies[2:2 + 2 * twos:2]
    margin = jnp.minimum(donor - 1, reach - receiver)
    shifted = jax.random.randint(jax.random.fold_in(key, 1), (twos,), 0, 1 << 20) % (margin + 1)
    tallies = tallies.at[1:1 + 2 * twos:2].set(donor - shifted).at[2:2 + 2 * twos:2].set(receiver + shifted)
    return tallies[jax.random.permutation(jax.random.fold_in(key, 2), number_of)]


def scatter_about(rng, dims, spread, reach, cuts=(), kind=jnp.bfloat16):
    gain = block_levels(rng, dims, cuts, -0.22, 0.18) if cuts else 1.0
    array = jax.random.normal(rng, dims, jnp.float32) * spread * gain
    return jnp.minimum(jnp.maximum(array, -reach), reach).astype(kind)


def setup_inputs(seed: int = 0) -> dict:
    streams_of = jax.random.split(jax.random.key(seed), 12)
    return {
        "tokens": scatter_about(streams_of[0], (SEQS, SEQ, D), 1.0, 6.0, ((0, 32),)),
        "segments": jax.vmap(lambda own: jnp.searchsorted(jnp.cumsum(uneven(own, SEQ // 4, SEQ, SEQ // 2, 2)), jnp.arange(SEQ), side="right"))(jax.random.split(streams_of[1], SEQS)).reshape((SEQS, SEQ)).astype(jnp.int32),
        "norm1_gain": jnp.clip(1.0 + 0.1 * jax.random.normal(streams_of[2], (D,), jnp.float32), 0.5, 1.5).astype(jnp.bfloat16),
        "qkv_weight": scatter_about(streams_of[3], (D, QKV), D ** -0.5, 0.1875, ((0, 2),)),
        "qkv_bias": draw_qkv_bias(jax.random.fold_in(streams_of[11], 71), 0),
        "out_weight": scatter_about(streams_of[5], (HQ, D), (HQ // 4) ** -0.5, 0.375, ((0, 2),)),
        "norm2_gain": jnp.clip(1.0 + 0.1 * jax.random.normal(streams_of[6], (D,), jnp.float32), 0.5, 1.5).astype(jnp.bfloat16),
        "gate_weight": scatter_about(streams_of[7], (D, FF), D ** -0.5, 0.1875, ((1, 2),)),
        "up_weight": scatter_about(streams_of[8], (D, FF), D ** -0.5, 0.1875, ((1, 2),)),
        "down_weight": scatter_about(streams_of[9], (FF, D), FF ** -0.5, 0.078125, ((0, 2),)),
        "cotangent": scatter_about(streams_of[10], (SEQS, SEQ, D), 1.0, 6.0, ((0, 32),)),
    }


EPSILON = 1e-06
ROPE_BASE = 1000000.0
NEG_LARGE = -1e+30

def doc_layout(segments, head_dim):
    length = segments.shape[1]
    places = jnp.arange(length, dtype=jnp.int32)
    same_doc = segments[:, :, None] == segments[:, None, :]
    earlier = places[None, None, :] < places[None, :, None]
    positions = lax.optimization_barrier(jnp.sum(jnp.where(same_doc & earlier, 1.0, 0.0).astype(jnp.float32), axis=2))
    allowed = jnp.where(same_doc & (places[None, None, :] <= places[None, :, None]), 1, 0).astype(jnp.int32)
    half_dim = head_dim // 2
    frequency = ROPE_BASE ** (-2.0 * jnp.arange(half_dim, dtype=jnp.float32) / head_dim)
    angles = positions[:, :, None] * frequency[None, None, :]
    return (allowed, jnp.cos(angles)[:, :, None, :], jnp.sin(angles)[:, :, None, :])

def rotate(values, cosine, sine):
    half_dim = values.shape[-1] // 2
    front_half = values[..., :half_dim]
    back_half = values[..., half_dim:]
    return jnp.concatenate([front_half * cosine - back_half * sine, back_half * cosine + front_half * sine], axis=-1)

def unrotate(gradients, cosine, sine):
    half_dim = gradients.shape[-1] // 2
    front_half = gradients[..., :half_dim]
    back_half = gradients[..., half_dim:]
    return jnp.concatenate([front_half * cosine + back_half * sine, back_half * cosine - front_half * sine], axis=-1)

def inverse_rms(hidden):
    return lax.rsqrt(lax.optimization_barrier(jnp.mean(hidden * hidden, axis=-1, keepdims=True)) + EPSILON)

def norm_backward(hidden, inv_rms, gain_f, back_normed):
    weighted = back_normed * gain_f
    inner = lax.optimization_barrier(jnp.mean(weighted * hidden, axis=-1, keepdims=True))
    back_hidden = inv_rms * weighted - hidden * (inv_rms * inv_rms * inv_rms) * inner
    back_gain = lax.optimization_barrier(jnp.sum(back_normed * hidden * inv_rms, axis=0))
    return (back_hidden, back_gain)

def matmul(left, right):
    return jnp.dot(left, right, preferred_element_type=jnp.float32)

def outer_sum(left, right):
    return lax.dot_general(left, right, (((0,), (0,)), ((), ())), preferred_element_type=jnp.float32)

def times_transposed(left, right):
    return lax.dot_general(left, right, (((1,), (1,)), ((), ())), preferred_element_type=jnp.float32)

def score_block(query_b, keys_b, allowed, score_scale):
    scores = jnp.einsum('sqkgd,spkd->skgqp', query_b.astype(jnp.float32), keys_b.astype(jnp.float32)) * score_scale
    return jnp.where(allowed[:, None, None, :, :] > 0, scores, NEG_LARGE)

def block_pass(tokens, segments, cotangent, params):
    norm1_gain, qkv_weight, qkv_bias, out_weight, norm2_gain, gate_weight, up_weight, down_weight = params
    sequences, length, model_width = tokens.shape
    row_count = sequences * length
    q_width = H * HD
    kv_width = KV * HD
    groups = H // KV
    score_scale = HD ** (-0.5)
    allowed, cosine, sine = doc_layout(segments, HD)
    resid_in = tokens.reshape(row_count, model_width).astype(jnp.float32)
    inv_rms1 = inverse_rms(resid_in)
    gain1 = norm1_gain.astype(jnp.float32)
    normed1 = (resid_in * inv_rms1 * gain1).astype(jnp.bfloat16)
    projected = matmul(normed1, qkv_weight) + qkv_bias.astype(jnp.float32)
    query = projected[:, :q_width].reshape(sequences, length, H, HD)
    keys_raw = projected[:, q_width:q_width + kv_width].reshape(sequences, length, KV, HD)
    values_raw = projected[:, q_width + kv_width:].reshape(sequences, length, KV, HD)
    query_b = rotate(query, cosine, sine).astype(jnp.bfloat16).reshape(sequences, length, KV, groups, HD)
    keys_b = rotate(keys_raw, cosine, sine).astype(jnp.bfloat16)
    values_b = values_raw.astype(jnp.bfloat16)
    scores = score_block(query_b, keys_b, allowed, score_scale)
    top_score = lax.optimization_barrier(jnp.max(scores, axis=-1, keepdims=True))
    log_total = top_score + jnp.log(lax.optimization_barrier(jnp.sum(jnp.exp(scores - top_score), axis=-1, keepdims=True)))
    soft = jnp.exp(scores - log_total)
    soft_b = soft.astype(jnp.bfloat16)
    context = jnp.einsum('skgqp,spkd->sqkgd', soft_b.astype(jnp.float32), values_b.astype(jnp.float32))
    context_b = context.astype(jnp.bfloat16).reshape(row_count, q_width)
    middle = resid_in + matmul(context_b, out_weight)
    inv_rms2 = inverse_rms(middle)
    gain2 = norm2_gain.astype(jnp.float32)
    normed2 = (middle * inv_rms2 * gain2).astype(jnp.bfloat16)
    gate_pre = matmul(normed2, gate_weight)
    up_proj = matmul(normed2, up_weight)
    sigmoid_gate = jax.nn.sigmoid(gate_pre)
    silu_gate = gate_pre * sigmoid_gate
    activ_b = (silu_gate * up_proj).astype(jnp.bfloat16)
    result = middle + matmul(activ_b, down_weight)
    back_rows = cotangent.reshape(row_count, model_width)
    back_activ = times_transposed(back_rows, down_weight)
    back_gate = (back_activ * up_proj * sigmoid_gate * (1.0 + gate_pre * (1.0 - sigmoid_gate))).astype(jnp.bfloat16)
    back_up = (back_activ * silu_gate).astype(jnp.bfloat16)
    grad_down = outer_sum(activ_b, back_rows)
    grad_gate = outer_sum(normed2, back_gate)
    grad_up = outer_sum(normed2, back_up)
    back_normed2 = times_transposed(back_gate, gate_weight) + times_transposed(back_up, up_weight)
    back_norm2, grad_norm2 = norm_backward(middle, inv_rms2, gain2, back_normed2)
    back_middle = back_rows.astype(jnp.float32) + back_norm2
    back_middle_b = back_middle.astype(jnp.bfloat16)
    grad_out = outer_sum(context_b, back_middle_b)
    back_context = times_transposed(back_middle_b, out_weight).astype(jnp.bfloat16)
    back_context = back_context.reshape(sequences, length, KV, groups, HD).astype(jnp.float32)
    back_values = jnp.einsum('skgqp,sqkgd->spkd', soft_b.astype(jnp.float32), back_context)
    back_soft = jnp.einsum('sqkgd,spkd->skgqp', back_context, values_b.astype(jnp.float32))
    row_dot = lax.optimization_barrier(jnp.sum(soft * back_soft, axis=-1, keepdims=True))
    back_scores = (soft * (back_soft - row_dot) * score_scale).astype(jnp.bfloat16).astype(jnp.float32)
    back_query = jnp.einsum('skgqp,spkd->sqkgd', back_scores, keys_b.astype(jnp.float32))
    back_keys = jnp.einsum('skgqp,sqkgd->spkd', back_scores, query_b.astype(jnp.float32))
    back_query = unrotate(back_query.reshape(sequences, length, H, HD), cosine, sine)
    back_keys = unrotate(back_keys, cosine, sine)
    back_proj = jnp.concatenate([back_query.reshape(row_count, q_width), back_keys.reshape(row_count, kv_width), back_values.reshape(row_count, kv_width)], axis=1)
    grad_bias = lax.optimization_barrier(jnp.sum(back_proj, axis=0))
    back_proj_b = back_proj.astype(jnp.bfloat16)
    grad_qkv = outer_sum(normed1, back_proj_b)
    back_normed1 = times_transposed(back_proj_b, qkv_weight)
    back_norm1, grad_norm1 = norm_backward(resid_in, inv_rms1, gain1, back_normed1)
    back_tokens = back_middle + back_norm1
    shape_out = (sequences, length, model_width)
    gradients = (grad_norm1, grad_qkv, grad_bias, grad_out, grad_norm2, grad_gate, grad_up, grad_down)
    return (result.reshape(shape_out), back_tokens.reshape(shape_out), gradients)

def reference(tokens, segments, norm1_gain, qkv_weight, qkv_bias, out_weight, norm2_gain, gate_weight, up_weight, down_weight, cotangent):
    params = (norm1_gain, qkv_weight, qkv_bias, out_weight, norm2_gain, gate_weight, up_weight, down_weight)
    block_seqs = 32 if SEQS % 32 == 0 else SEQS
    block_count = SEQS // block_seqs
    tok_blocks = tokens.reshape(block_count, block_seqs, SEQ, D)
    seg_blocks = segments.reshape(block_count, block_seqs, SEQ)
    cot_blocks = cotangent.reshape(block_count, block_seqs, SEQ, D)
    start = tuple((jnp.zeros(weight.shape, jnp.float32) for weight in params))

    def advance(carry, pieces):
        tok_piece, seg_piece, cot_piece = pieces
        result_piece, back_piece, gradients = block_pass(tok_piece, seg_piece, cot_piece, params)
        return (jax.tree.map(jnp.add, carry, gradients), (result_piece, back_piece))
    totals, outputs = lax.scan(advance, start, (tok_blocks, seg_blocks, cot_blocks))
    result = outputs[0].reshape(SEQS, SEQ, D)
    back_tokens = outputs[1].reshape(SEQS, SEQ, D)
    return (result, back_tokens, totals[0], totals[1], totals[2], totals[3], totals[4], totals[5], totals[6], totals[7])
```

```python
import functools

import jax
import jax.numpy as jnp
from jax import lax
from jax.experimental import pallas as pl
from jax.experimental.pallas import tpu as pltpu
from jax.sharding import PartitionSpec as P

H = 14
KV = 2
HD = 64


EPSILON = 1e-06
ROPE_BASE = 1000000.0
NEG_LARGE = -1e30


def doc_layout(segments, head_dim):
    length = segments.shape[1]
    places = jnp.arange(length, dtype=jnp.int32)
    same_doc = segments[:, :, None] == segments[:, None, :]
    earlier = places[None, None, :] < places[None, :, None]
    positions = jnp.sum(jnp.where(same_doc & earlier, 1.0, 0.0).astype(jnp.float32), axis=2)
    allowed = jnp.where(same_doc & (places[None, None, :] <= places[None, :, None]), 1, 0).astype(
        jnp.int32
    )
    half_dim = head_dim // 2
    frequency = ROPE_BASE ** (-2.0 * jnp.arange(half_dim, dtype=jnp.float32) / head_dim)
    angles = positions[:, :, None] * frequency[None, None, :]
    return (allowed, jnp.cos(angles)[:, :, None, :], jnp.sin(angles)[:, :, None, :])


def rotate(values, cosine, sine):
    half_dim = values.shape[-1] // 2
    front_half = values[..., :half_dim]
    back_half = values[..., half_dim:]
    return jnp.concatenate(
        [front_half * cosine - back_half * sine, back_half * cosine + front_half * sine], axis=-1
    )


def unrotate(gradients, cosine, sine):
    half_dim = gradients.shape[-1] // 2
    front_half = gradients[..., :half_dim]
    back_half = gradients[..., half_dim:]
    return jnp.concatenate(
        [front_half * cosine + back_half * sine, back_half * cosine - front_half * sine], axis=-1
    )


def inverse_rms(hidden):
    return lax.rsqrt(jnp.mean(hidden * hidden, axis=-1, keepdims=True) + EPSILON)


def norm_backward(hidden, inv_rms, gain_f, back_normed):
    weighted = back_normed * gain_f
    inner = jnp.mean(weighted * hidden, axis=-1, keepdims=True)
    back_hidden = inv_rms * weighted - hidden * (inv_rms * inv_rms * inv_rms) * inner
    back_gain = jnp.sum(back_normed * hidden * inv_rms, axis=0)
    return (back_hidden, back_gain)


def matmul(left, right):
    return jnp.dot(left, right, preferred_element_type=jnp.float32)


def outer_sum(left, right):
    return lax.dot_general(
        left, right, (((0,), (0,)), ((), ())), preferred_element_type=jnp.float32
    )


def times_transposed(left, right):
    return lax.dot_general(
        left, right, (((1,), (1,)), ((), ())), preferred_element_type=jnp.float32
    )


def score_block(query_b, keys_b, allowed, score_scale):
    scores = (
        jnp.einsum("sqkgd,spkd->skgqp", query_b, keys_b, preferred_element_type=jnp.float32)
        * score_scale
    )
    return jnp.where(allowed[:, None, None, :, :] > 0, scores, NEG_LARGE)


def stage_bits(copies, far_first):
    bits = [1 << i for i in range(copies.bit_length() - 1)]
    if far_first:
        bits = bits[:1] + bits[2:] + bits[1:2]
    return bits


def sum_kernel(copies, pieces, count, *refs):
    ins, outs = refs[:count], refs[count : 2 * count]
    n = len(pieces)
    held = refs[2 * count : 2 * count + n]
    landed = refs[2 * count + n : 2 * count + 2 * n]
    final = refs[2 * count + 2 * n : 2 * count + 3 * n]
    send_sem, recv_sem, local_sem = refs[2 * count + 3 * n :]
    me = lax.axis_index("replica")
    stages = copies.bit_length() - 1

    def partner(bit):
        return me + bit * (1 - 2 * (lax.div(me, bit) % 2))

    loads = []
    for p, (which, start, width, _) in enumerate(pieces):
        load = pltpu.make_async_copy(
            ins[which].at[:, :, pl.ds(start, width)], held[p], local_sem.at[p, 0]
        )
        load.start()
        loads.append(load)
    barrier = pltpu.get_barrier_semaphore()
    for i in range(stages):
        pl.semaphore_signal(
            barrier,
            inc=1,
            device_id={"replica": partner(1 << i)},
            device_id_type=pl.DeviceIdType.MESH,
        )
    pl.semaphore_wait(barrier, stages)

    bits = [stage_bits(copies, far) for (_, _, _, far) in pieces]
    base = [0] * n
    trail = [[] for _ in range(n)]
    copying = [None] * n
    for k in range(stages + 1):
        size = copies >> (k + 1)
        offset = copies - (copies >> k)
        for p in range(n):
            if k == 0:
                loads[p].wait()
            else:
                copying[p].wait()
                old, previous = copies >> k, copies - (copies >> (k - 1))
                first = base[p]

                goal = held[p] if k < stages else final[p]

                def add(i, carry, p=p, goal=goal, first=first, previous=previous):
                    goal[first + i] = held[p][first + i] + landed[p][previous + i]
                    return carry

                lax.fori_loop(0, old, add, 0)
            if k < stages:
                bit = bits[p][k]
                side = lax.div(me, bit) % 2
                keep, give = base[p] + side * size, base[p] + (1 - side) * size
                copy = pltpu.make_async_remote_copy(
                    src_ref=held[p].at[pl.ds(give, size)],
                    dst_ref=landed[p].at[pl.ds(offset, size)],
                    send_sem=send_sem.at[p, k],
                    recv_sem=recv_sem.at[p, k],
                    device_id={"replica": partner(bit)},
                    device_id_type=pl.DeviceIdType.MESH,
                )
                trail[p].append(keep)
                base[p] = keep
            else:
                copy = spread(final, send_sem, recv_sem, trail, bits, partner, p, k - 1, copies)
            copy.start()
            copying[p] = copy
    stores = []
    for k in range(stages - 1, -1, -1):
        for p, (which, start, width, _) in enumerate(pieces):
            copying[p].wait()
            if k > 0:
                copying[p] = spread(
                    final, send_sem, recv_sem, trail, bits, partner, p, k - 1, copies
                )
                copying[p].start()
            else:
                store = pltpu.make_async_copy(
                    final[p], outs[which].at[:, :, pl.ds(start, width)], local_sem.at[p, 1]
                )
                store.start()
                stores.append(store)
    for store in stores:
        store.wait()


def spread(final, send_sem, recv_sem, trail, bits, partner, p, k, copies):
    block = final[p].at[pl.ds(trail[p][k], copies >> (k + 1))]
    stages = copies.bit_length() - 1
    return pltpu.make_async_remote_copy(
        src_ref=block,
        dst_ref=block,
        send_sem=send_sem.at[p, stages + k],
        recv_sem=recv_sem.at[p, stages + k],
        device_id={"replica": partner(bits[p][k])},
        device_id_type=pl.DeviceIdType.MESH,
    )


def replica_sum(arrays, copies):
    pieces = []
    for which, array in enumerate(arrays):
        columns = array.shape[2]
        cut = -(-columns // 256) * 128
        if columns > 1024:
            pieces += [(which, 0, cut, False), (which, cut, columns - cut, True)]
        else:
            half = columns // 256 * 128
            pieces += [(which, 0, half, True), (which, half, columns - half, False)]
    stages = copies.bit_length() - 1
    n, count = len(pieces), len(arrays)
    shapes = [(arrays[w].shape[1], width) for (w, _, width, _) in pieces]
    any_spec = pl.BlockSpec(memory_space=pltpu.HBM)
    return pl.pallas_call(
        functools.partial(sum_kernel, copies, tuple(pieces), count),
        out_shape=[jax.ShapeDtypeStruct(a.shape, a.dtype) for a in arrays],
        in_specs=[any_spec] * count,
        out_specs=[any_spec] * count,
        scratch_shapes=[pltpu.VMEM((copies, r, c), jnp.bfloat16) for r, c in shapes]
        + [pltpu.VMEM((copies - 1, r, c), jnp.bfloat16) for r, c in shapes]
        + [pltpu.VMEM((copies, r, c), jnp.bfloat16) for r, c in shapes]
        + [
            pltpu.SemaphoreType.DMA((n, 2 * stages)),
            pltpu.SemaphoreType.DMA((n, 2 * stages)),
            pltpu.SemaphoreType.DMA((n, 2)),
        ],
        compiler_params=pltpu.CompilerParams(
            collective_id=0, has_side_effects=True, vmem_limit_bytes=52 * 1024 * 1024
        ),
        name="replica_sum",
    )(*arrays)


def swap(values):
    return lax.ppermute(values, "group", [(0, 1), (1, 0)])


def gather_weight(shard, pairs, copies):
    if pairs != 2 or copies % 2:
        return lax.all_gather(shard, "group", axis=0, tiled=True)
    half = shard.shape[0] // 2
    core = lax.axis_index("replica") % 2
    mine = swap(lax.dynamic_slice_in_dim(shard, core * half, half, 0))
    sibling = lax.ppermute(mine, "replica", [(i, i + 1 - 2 * (i % 2)) for i in range(copies)])
    front = jnp.where(core == 0, mine, sibling)
    back = jnp.where(core == 0, sibling, mine)
    first = lax.axis_index("group") == 0
    other = jnp.concatenate([front, back], axis=0)
    return jnp.concatenate(
        [jnp.where(first, shard, other), jnp.where(first, other, shard)], axis=0
    )


def gather_vectors(vectors, pairs):
    if pairs != 2:
        return [lax.all_gather(v, "group", axis=0, tiled=True) for v in vectors]
    joined = jnp.concatenate(vectors)
    other = swap(joined)
    first = lax.axis_index("group") == 0
    low, high = jnp.where(first, joined, other), jnp.where(first, other, joined)
    found, at = [], 0
    for v in vectors:
        size = v.shape[0]
        found.append(jnp.concatenate([low[at : at + size], high[at : at + size]]))
        at += size
    return found


def gather_rows(rows, pairs):
    if pairs != 2:
        return lax.all_gather(rows, "group", axis=0, tiled=True)
    return jnp.concatenate([rows, swap(rows)], axis=0)


def scatter_rows(partial, pairs):
    if pairs != 2:
        return lax.psum_scatter(
            partial.astype(jnp.bfloat16), "group", scatter_dimension=0, tiled=True
        ).astype(jnp.float32)
    half = partial.shape[0] // 2
    return partial[:half] + swap(partial[half:].astype(jnp.bfloat16)).astype(jnp.float32)


def scatter_owned(partial, pairs):
    if pairs != 2:
        return lax.psum_scatter(
            partial.astype(jnp.bfloat16), "group", scatter_dimension=0, tiled=True
        ).astype(jnp.float32)
    half = partial.shape[0] // 2
    me = lax.axis_index("group")
    give = lax.dynamic_slice_in_dim(partial.astype(jnp.bfloat16), (1 - me) * half, half, 0)
    keep = lax.dynamic_slice_in_dim(partial, me * half, half, 0)
    return keep + swap(give).astype(jnp.float32)


def sum_owned(small, qkv, out, gate, up, down, copies):
    rows, width = qkv.shape[0], qkv.shape[1] + out.shape[1]
    lines = 64
    fits = (
        copies == 16
        and width % 256 == 0
        and rows + 64 == copies // 2 * 64
        and small.shape[0] <= width
        and all(a.shape[0] % (8 * copies) == 0 and a.shape[1] % 128 == 0 for a in (gate, up, down))
    )
    if not fits:
        return lax.psum(
            tuple(a.astype(jnp.bfloat16) for a in (small, qkv, out, gate, up, down)), "replica"
        )
    joined = jnp.concatenate([qkv, out], axis=1)
    line = jnp.pad(small, (0, width - small.shape[0]))[None, :]
    joined = jnp.concatenate(
        [joined, jnp.pad(line, ((0, lines - 1), (0, 0)))], axis=0
    ).astype(jnp.bfloat16)
    half = width // 2
    joined = jnp.stack([joined[:, :half], joined[:, half:]]).reshape(copies, lines, half)
    folded = [
        a.astype(jnp.bfloat16).reshape(copies, a.shape[0] // copies, a.shape[1])
        for a in (gate, up, down)
    ]
    gate_s, up_s, down_s, joined = replica_sum([*folded, joined], copies)
    joined = joined.reshape(2, rows + lines, half)
    joined = jnp.concatenate([joined[0], joined[1]], axis=1)
    return (
        joined[rows, : small.shape[0]],
        joined[:rows, : qkv.shape[1]],
        joined[:rows, qkv.shape[1] :],
        gate_s.reshape(gate.shape),
        up_s.reshape(up.shape),
        down_s.reshape(down.shape),
    )


def on_device(
    tokens,
    segments,
    norm1_gain,
    qkv_weight,
    qkv_bias,
    out_weight,
    norm2_gain,
    gate_weight,
    up_weight,
    down_weight,
    cotangent,
    *,
    pairs,
    copies,
):
    sequences, length, model_width = tokens.shape
    row_count = sequences * length
    q_width = H * HD
    kv_width = KV * HD
    groups = H // KV
    score_scale = HD ** (-0.5)
    gain1_b, b_qkv, gain2_b = gather_vectors([norm1_gain, qkv_bias, norm2_gain], pairs)
    w_qkv = gather_weight(qkv_weight, pairs, copies)
    back_all = gather_rows(cotangent.reshape(row_count, model_width), pairs)
    w_out = gather_weight(out_weight, pairs, copies)
    allowed, cosine, sine = doc_layout(segments, HD)
    resid_in = tokens.reshape(row_count, model_width).astype(jnp.float32)
    inv_rms1 = inverse_rms(resid_in)
    gain1 = gain1_b.astype(jnp.float32)
    normed1 = (resid_in * inv_rms1 * gain1).astype(jnp.bfloat16)
    projected = matmul(normed1, w_qkv) + b_qkv.astype(jnp.float32)
    query = projected[:, :q_width].reshape(sequences, length, H, HD)
    keys_raw = projected[:, q_width : q_width + kv_width].reshape(sequences, length, KV, HD)
    values_raw = projected[:, q_width + kv_width :].reshape(sequences, length, KV, HD)
    query_b = (
        rotate(query, cosine, sine).astype(jnp.bfloat16).reshape(sequences, length, KV, groups, HD)
    )
    keys_b = rotate(keys_raw, cosine, sine).astype(jnp.bfloat16)
    values_b = values_raw.astype(jnp.bfloat16)
    scores = score_block(query_b, keys_b, allowed, score_scale)
    top_score = jnp.max(scores, axis=-1, keepdims=True)
    log_total = top_score + jnp.log(jnp.sum(jnp.exp(scores - top_score), axis=-1, keepdims=True))
    soft_b = jnp.exp(scores - log_total).astype(jnp.bfloat16)
    context = jnp.einsum("skgqp,spkd->sqkgd", soft_b, values_b, preferred_element_type=jnp.float32)
    context_b = context.astype(jnp.bfloat16).reshape(row_count, q_width)
    middle = resid_in + matmul(context_b, w_out)
    inv_rms2 = inverse_rms(middle)
    gain2 = gain2_b.astype(jnp.float32)
    normed2 = (middle * inv_rms2 * gain2).astype(jnp.bfloat16)
    back_rows = cotangent.reshape(row_count, model_width)
    normed_all = gather_rows(normed2, pairs)
    gate_pre = matmul(normed_all, gate_weight)
    up_proj = matmul(normed_all, up_weight)
    sigmoid_gate = jax.nn.sigmoid(gate_pre)
    silu_gate = gate_pre * sigmoid_gate
    activ_b = (silu_gate * up_proj).astype(jnp.bfloat16)
    result = middle + scatter_rows(matmul(activ_b, down_weight), pairs)
    back_activ = times_transposed(back_all, down_weight)
    back_gate = (
        back_activ * up_proj * sigmoid_gate * (1.0 + gate_pre * (1.0 - sigmoid_gate))
    ).astype(jnp.bfloat16)
    back_up = (back_activ * silu_gate).astype(jnp.bfloat16)
    grad_down = outer_sum(activ_b, back_all)
    grad_gate = outer_sum(normed_all, back_gate)
    grad_up = outer_sum(normed_all, back_up)
    local_normed = times_transposed(back_gate, gate_weight) + times_transposed(back_up, up_weight)
    back_normed2 = scatter_rows(local_normed, pairs)
    back_norm2, grad_norm2_part = norm_backward(middle, inv_rms2, gain2, back_normed2)
    back_middle = back_rows.astype(jnp.float32) + back_norm2
    back_middle_b = back_middle.astype(jnp.bfloat16)
    grad_out_part = outer_sum(context_b, back_middle_b)
    back_context = times_transposed(back_middle_b, w_out).astype(jnp.bfloat16)
    back_context = back_context.reshape(sequences, length, KV, groups, HD)
    soft = jnp.exp(score_block(query_b, keys_b, allowed, score_scale) - log_total)
    soft_again = soft.astype(jnp.bfloat16)
    back_values = jnp.einsum(
        "skgqp,sqkgd->spkd", soft_again, back_context, preferred_element_type=jnp.float32
    )
    back_soft = jnp.einsum(
        "sqkgd,spkd->skgqp", back_context, values_b, preferred_element_type=jnp.float32
    )
    row_dot = jnp.sum(soft * back_soft, axis=-1, keepdims=True)
    back_scores = (soft * (back_soft - row_dot) * score_scale).astype(jnp.bfloat16)
    back_query = jnp.einsum(
        "skgqp,spkd->sqkgd", back_scores, keys_b, preferred_element_type=jnp.float32
    )
    back_keys = jnp.einsum(
        "skgqp,sqkgd->spkd", back_scores, query_b, preferred_element_type=jnp.float32
    )
    back_query = unrotate(back_query.reshape(sequences, length, H, HD), cosine, sine)
    back_keys = unrotate(back_keys, cosine, sine)
    back_proj = jnp.concatenate(
        [
            back_query.reshape(row_count, q_width),
            back_keys.reshape(row_count, kv_width),
            back_values.reshape(row_count, kv_width),
        ],
        axis=1,
    )
    grad_bias_part = jnp.sum(back_proj, axis=0)
    back_proj_b = back_proj.astype(jnp.bfloat16)
    grad_qkv_part = outer_sum(normed1, back_proj_b)
    back_normed1 = times_transposed(back_proj_b, w_qkv)
    back_norm1, grad_norm1_part = norm_backward(resid_in, inv_rms1, gain1, back_normed1)
    back_tokens = back_middle + back_norm1
    small = jnp.stack([v.reshape(pairs, -1) for v in (grad_norm1_part, grad_norm2_part)], axis=1)
    small = jnp.concatenate(
        [small.reshape(pairs, -1), grad_bias_part.reshape(pairs, -1)], axis=1
    ).reshape(-1)
    small = scatter_owned(small, pairs)
    owned = sum_owned(
        small,
        scatter_owned(grad_qkv_part, pairs),
        scatter_owned(grad_out_part, pairs),
        grad_gate,
        grad_up,
        grad_down,
        copies,
    )
    small, grad_qkv, grad_out, grad_gate, grad_up, grad_down = (
        a.astype(jnp.float32) for a in owned
    )
    gains = norm1_gain.shape[0]
    grad_norm1, grad_norm2, grad_bias = (
        small[:gains],
        small[gains : 2 * gains],
        small[2 * gains :],
    )
    shape_out = (sequences, length, model_width)
    return (
        result.reshape(shape_out),
        back_tokens.reshape(shape_out),
        grad_norm1,
        grad_qkv,
        grad_bias,
        grad_out,
        grad_norm2,
        grad_gate,
        grad_up,
        grad_down,
    )


def solution(mesh):
    in_specs = (
        P(("group", "replica"), None, None),
        P(("group", "replica"), None),
        P("group"),
        P("group", None),
        P("group"),
        P("group", None),
        P("group"),
        P(None, "group"),
        P(None, "group"),
        P("group", None),
        P(("group", "replica"), None, None),
    )
    out_specs = (
        P(("group", "replica"), None, None),
        P(("group", "replica"), None, None),
        P("group"),
        P("group", None),
        P("group"),
        P("group", None),
        P("group"),
        P(None, "group"),
        P(None, "group"),
        P("group", None),
    )
    program = functools.partial(
        on_device, pairs=mesh.shape["group"], copies=mesh.shape["replica"]
    )
    return jax.shard_map(
        program, mesh=mesh, in_specs=in_specs, out_specs=out_specs, check_vma=False
    )
```

```python
import functools

import jax
import jax.numpy as jnp
from jax import lax
from jax.experimental import pallas as pl
from jax.experimental.pallas import tpu as pltpu
from jax.sharding import PartitionSpec as P

H = 14
KV = 2
HD = 64


EPSILON = 1e-06
ROPE_BASE = 1000000.0
NEG_LARGE = -1e30


def doc_layout(segments, head_dim):
    length = segments.shape[1]
    places = jnp.arange(length, dtype=jnp.int32)
    same_doc = segments[:, :, None] == segments[:, None, :]
    earlier = places[None, None, :] < places[None, :, None]
    positions = jnp.sum(jnp.where(same_doc & earlier, 1.0, 0.0).astype(jnp.float32), axis=2)
    allowed = jnp.where(same_doc & (places[None, None, :] <= places[None, :, None]), 1, 0).astype(
        jnp.int32
    )
    half_dim = head_dim // 2
    frequency = ROPE_BASE ** (-2.0 * jnp.arange(half_dim, dtype=jnp.float32) / head_dim)
    angles = positions[:, :, None] * frequency[None, None, :]
    return (allowed, jnp.cos(angles)[:, :, None, :], jnp.sin(angles)[:, :, None, :])


def rotate(values, cosine, sine):
    half_dim = values.shape[-1] // 2
    front_half = values[..., :half_dim]
    back_half = values[..., half_dim:]
    return jnp.concatenate(
        [front_half * cosine - back_half * sine, back_half * cosine + front_half * sine], axis=-1
    )


def unrotate(gradients, cosine, sine):
    half_dim = gradients.shape[-1] // 2
    front_half = gradients[..., :half_dim]
    back_half = gradients[..., half_dim:]
    return jnp.concatenate(
        [front_half * cosine + back_half * sine, back_half * cosine - front_half * sine], axis=-1
    )


def inverse_rms(hidden):
    return lax.rsqrt(jnp.mean(hidden * hidden, axis=-1, keepdims=True) + EPSILON)


def norm_backward(hidden, inv_rms, gain_f, back_normed):
    weighted = back_normed * gain_f
    inner = jnp.mean(weighted * hidden, axis=-1, keepdims=True)
    back_hidden = inv_rms * weighted - hidden * (inv_rms * inv_rms * inv_rms) * inner
    back_gain = jnp.sum(back_normed * hidden * inv_rms, axis=0)
    return (back_hidden, back_gain)


def matmul(left, right):
    return jnp.dot(left, right, preferred_element_type=jnp.float32)


def outer_sum(left, right):
    return lax.dot_general(
        left, right, (((0,), (0,)), ((), ())), preferred_element_type=jnp.float32
    )


def times_transposed(left, right):
    return lax.dot_general(
        left, right, (((1,), (1,)), ((), ())), preferred_element_type=jnp.float32
    )


def score_block(query_b, keys_b, allowed, score_scale):
    scores = (
        jnp.einsum("sqkgd,spkd->skgqp", query_b, keys_b, preferred_element_type=jnp.float32)
        * score_scale
    )
    return jnp.where(allowed[:, None, None, :, :] > 0, scores, NEG_LARGE)


def stage_bits(copies, far_first):
    bits = [1 << i for i in range(copies.bit_length() - 1)]
    if far_first:
        bits = bits[:1] + bits[2:] + bits[1:2]
    return bits


def sum_kernel(copies, pieces, swapped, count, *refs):
    ins, outs = refs[:count], refs[count : 2 * count]
    n = len(pieces)
    held = refs[2 * count : 2 * count + n]
    landed = refs[2 * count + n : 2 * count + 2 * n]
    final = refs[2 * count + 2 * n : 2 * count + 3 * n]
    extra = refs[2 * count + 3 * n : -3]
    send_sem, recv_sem, local_sem = refs[-3:]
    me = lax.axis_index("replica")
    pair = lax.axis_index("group")
    stages = copies.bit_length() - 1
    mesh_id = pl.DeviceIdType.MESH

    def partner(bit):
        return me + bit * (1 - 2 * (lax.div(me, bit) % 2))

    loads = []
    for p, (which, start, width, _, _) in enumerate(pieces):
        source = ins[which].at[pair] if which == swapped else ins[which]
        load = pltpu.make_async_copy(
            source.at[:, :, pl.ds(start, width)], held[p], local_sem.at[p, 0]
        )
        load.start()
        loads.append(load)
    barrier = pltpu.get_barrier_semaphore()
    for i in range(stages):
        pl.semaphore_signal(
            barrier, inc=1, device_id={"replica": partner(1 << i)}, device_id_type=mesh_id
        )
    pl.semaphore_signal(barrier, inc=1, device_id={"group": 1 - pair}, device_id_type=mesh_id)
    pl.semaphore_wait(barrier, stages + 1)

    swaps, at = {}, 0
    for p, (which, start, width, _, _) in enumerate(pieces):
        if which == swapped:
            copy = pltpu.make_async_remote_copy(
                src_ref=ins[which].at[1 - pair].at[:, :, pl.ds(start, width)],
                dst_ref=extra[at],
                send_sem=send_sem.at[p, 2 * stages],
                recv_sem=recv_sem.at[p, 2 * stages],
                device_id={"group": 1 - pair},
                device_id_type=mesh_id,
            )
            copy.start()
            swaps[p] = (copy, extra[at])
            at += 1

    bits = [stage_bits(copies, far) for (_, _, _, far, _) in pieces]
    base = [0] * n
    trail = [[] for _ in range(n)]
    copying = [None] * n
    stores = []

    def accumulate(goal, left, right, first, shift, size):
        def add(i, carry):
            goal[first + i] = left[first + i] + right[shift + i]
            return carry

        lax.fori_loop(0, size, add, 0)

    def spread(p, k):
        block = final[p].at[pl.ds(trail[p][k], copies >> (k + 1))]
        return pltpu.make_async_remote_copy(
            src_ref=block,
            dst_ref=block,
            send_sem=send_sem.at[p, stages + k],
            recv_sem=recv_sem.at[p, stages + k],
            device_id={"replica": partner(bits[p][k])},
            device_id_type=mesh_id,
        )

    def halve(p, k):
        size = copies >> (k + 1)
        bit = bits[p][k]
        side = lax.div(me, bit) % 2
        keep, give = base[p] + side * size, base[p] + (1 - side) * size
        trail[p].append(keep)
        base[p] = keep
        return pltpu.make_async_remote_copy(
            src_ref=held[p].at[pl.ds(give, size)],
            dst_ref=landed[p].at[pl.ds(copies - (copies >> k), size)],
            send_sem=send_sem.at[p, k],
            recv_sem=recv_sem.at[p, k],
            device_id={"replica": partner(bit)},
            device_id_type=mesh_id,
        )

    def step(p, k):
        if k == 0:
            loads[p].wait()
            if p in swaps:
                swaps[p][0].wait()
                accumulate(held[p], held[p], swaps[p][1], 0, 0, copies)
        else:
            copying[p].wait()
            if k <= stages:
                goal = held[p] if k < stages else final[p]
                shift = copies - (copies >> (k - 1))
                accumulate(goal, held[p], landed[p], base[p], shift, copies >> k)
        if k < stages:
            copying[p] = halve(p, k)
        elif k < 2 * stages:
            copying[p] = spread(p, 2 * stages - 1 - k)
        else:
            which, start, width, _, _ = pieces[p]
            store = pltpu.make_async_copy(
                final[p], outs[which].at[:, :, pl.ds(start, width)], local_sem.at[p, 1]
            )
            store.start()
            stores.append(store)
            return
        copying[p].start()

    for tick in range(2 * stages + 1 + max(piece[4] for piece in pieces)):
        for p in range(n):
            k = tick - pieces[p][4]
            if 0 <= k <= 2 * stages:
                step(p, k)
    for store in stores:
        store.wait()


def replica_sum(arrays, copies):
    swapped = len(arrays) - 1
    pieces = []
    for which, array in enumerate(arrays):
        columns = array.shape[-1]
        cut = columns // 256 * 128
        pieces += [(which, 0, cut, False, which), (which, cut, columns - cut, True, which)]
    stages = copies.bit_length() - 1
    n, count = len(pieces), len(arrays)
    shapes = [(arrays[w].shape[-2], width) for (w, _, width, _, _) in pieces]
    moved = [shape for shape, piece in zip(shapes, pieces) if piece[0] == swapped]
    any_spec = pl.BlockSpec(memory_space=pltpu.HBM)
    return pl.pallas_call(
        functools.partial(sum_kernel, copies, tuple(pieces), swapped, count),
        out_shape=[jax.ShapeDtypeStruct(a.shape[-3:], a.dtype) for a in arrays],
        in_specs=[any_spec] * count,
        out_specs=[any_spec] * count,
        scratch_shapes=[pltpu.VMEM((copies, r, c), jnp.bfloat16) for r, c in shapes]
        + [pltpu.VMEM((copies - 1, r, c), jnp.bfloat16) for r, c in shapes]
        + [pltpu.VMEM((copies, r, c), jnp.bfloat16) for r, c in shapes]
        + [pltpu.VMEM((copies, r, c), jnp.bfloat16) for r, c in moved]
        + [
            pltpu.SemaphoreType.DMA((n, 2 * stages + 1)),
            pltpu.SemaphoreType.DMA((n, 2 * stages + 1)),
            pltpu.SemaphoreType.DMA((n, 2)),
        ],
        compiler_params=pltpu.CompilerParams(
            collective_id=0, has_side_effects=True, vmem_limit_bytes=54 * 1024 * 1024
        ),
        name="replica_sum",
    )(*arrays)


def swap(values):
    return lax.ppermute(values, "group", [(0, 1), (1, 0)])


def gather_weight(shard, pairs, copies):
    if pairs != 2 or copies % 2:
        return lax.all_gather(shard, "group", axis=0, tiled=True)
    half = shard.shape[0] // 2
    core = lax.axis_index("replica") % 2
    mine = swap(lax.dynamic_slice_in_dim(shard, core * half, half, 0))
    sibling = lax.ppermute(mine, "replica", [(i, i + 1 - 2 * (i % 2)) for i in range(copies)])
    front = jnp.where(core == 0, mine, sibling)
    back = jnp.where(core == 0, sibling, mine)
    first = lax.axis_index("group") == 0
    other = jnp.concatenate([front, back], axis=0)
    return jnp.concatenate(
        [jnp.where(first, shard, other), jnp.where(first, other, shard)], axis=0
    )


def gather_vectors(vectors, pairs):
    if pairs != 2:
        return [lax.all_gather(v, "group", axis=0, tiled=True) for v in vectors]
    joined = jnp.concatenate(vectors)
    other = swap(joined)
    first = lax.axis_index("group") == 0
    low, high = jnp.where(first, joined, other), jnp.where(first, other, joined)
    found, at = [], 0
    for v in vectors:
        size = v.shape[0]
        found.append(jnp.concatenate([low[at : at + size], high[at : at + size]]))
        at += size
    return found


def gather_rows(rows, pairs):
    if pairs != 2:
        return lax.all_gather(rows, "group", axis=0, tiled=True)
    return jnp.concatenate([rows, swap(rows)], axis=0)


def scatter_rows(partial, pairs):
    if pairs != 2:
        return lax.psum_scatter(
            partial.astype(jnp.bfloat16), "group", scatter_dimension=0, tiled=True
        ).astype(jnp.float32)
    half = partial.shape[0] // 2
    return partial[:half] + swap(partial[half:].astype(jnp.bfloat16)).astype(jnp.float32)


def scatter_owned(partial):
    return lax.psum_scatter(
        partial.astype(jnp.bfloat16), "group", scatter_dimension=0, tiled=True
    ).astype(jnp.float32)


def sum_owned(small, qkv, out, gate, up, down, pairs, copies):
    rows, width = qkv.shape[0] // pairs, qkv.shape[1] + out.shape[1]
    share = small.shape[0] // pairs
    lines = 64
    fits = (
        copies == 16
        and pairs == 2
        and width % 256 == 0
        and rows + lines == copies // 2 * lines
        and share <= width
        and all(a.shape[0] % (8 * copies) == 0 and a.shape[1] % 128 == 0 for a in (gate, up, down))
    )
    if not fits:
        owned = [scatter_owned(a) for a in (small, qkv, out)]
        return lax.psum(
            tuple(a.astype(jnp.bfloat16) for a in (*owned, gate, up, down)), "replica"
        )
    half = width // 2
    joined = jnp.concatenate([qkv, out], axis=1).astype(jnp.bfloat16)
    joined = jnp.stack([joined[:, :half], joined[:, half:]])
    joined = joined.reshape(2, pairs, rows // lines, lines, half).transpose(1, 0, 2, 3, 4)
    small = small.astype(jnp.bfloat16).reshape(pairs, share)
    line = jnp.pad(small, ((0, 0), (0, width - share))).reshape(pairs, 2, 1, 1, half)
    line = jnp.pad(line, ((0, 0), (0, 0), (0, 0), (0, lines - 1), (0, 0)))
    joined = jnp.concatenate([joined, line], axis=2).reshape(pairs, copies, lines, half)
    folded = [
        a.astype(jnp.bfloat16).reshape(copies, a.shape[0] // copies, a.shape[1])
        for a in (gate, up, down)
    ]
    gate_s, up_s, down_s, joined = replica_sum([*folded, joined], copies)
    joined = joined.reshape(2, rows + lines, half)
    joined = jnp.concatenate([joined[0], joined[1]], axis=1)
    return (
        joined[rows, :share],
        joined[:rows, : qkv.shape[1]],
        joined[:rows, qkv.shape[1] :],
        gate_s.reshape(gate.shape),
        up_s.reshape(up.shape),
        down_s.reshape(down.shape),
    )


def on_device(
    tokens,
    segments,
    norm1_gain,
    qkv_weight,
    qkv_bias,
    out_weight,
    norm2_gain,
    gate_weight,
    up_weight,
    down_weight,
    cotangent,
    *,
    pairs,
    copies,
):
    sequences, length, model_width = tokens.shape
    row_count = sequences * length
    q_width = H * HD
    kv_width = KV * HD
    groups = H // KV
    score_scale = HD ** (-0.5)
    gain1_b, b_qkv, gain2_b = gather_vectors([norm1_gain, qkv_bias, norm2_gain], pairs)
    w_qkv = gather_weight(qkv_weight, pairs, copies)
    back_all = gather_rows(cotangent.reshape(row_count, model_width), pairs)
    w_out = gather_weight(out_weight, pairs, copies)
    allowed, cosine, sine = doc_layout(segments, HD)
    resid_in = tokens.reshape(row_count, model_width).astype(jnp.float32)
    inv_rms1 = inverse_rms(resid_in)
    gain1 = gain1_b.astype(jnp.float32)
    normed1 = (resid_in * inv_rms1 * gain1).astype(jnp.bfloat16)
    projected = matmul(normed1, w_qkv) + b_qkv.astype(jnp.float32)
    query = projected[:, :q_width].reshape(sequences, length, H, HD)
    keys_raw = projected[:, q_width : q_width + kv_width].reshape(sequences, length, KV, HD)
    values_raw = projected[:, q_width + kv_width :].reshape(sequences, length, KV, HD)
    query_b = (
        rotate(query, cosine, sine).astype(jnp.bfloat16).reshape(sequences, length, KV, groups, HD)
    )
    keys_b = rotate(keys_raw, cosine, sine).astype(jnp.bfloat16)
    values_b = values_raw.astype(jnp.bfloat16)
    scores = score_block(query_b, keys_b, allowed, score_scale)
    top_score = jnp.max(scores, axis=-1, keepdims=True)
    log_total = top_score + jnp.log(jnp.sum(jnp.exp(scores - top_score), axis=-1, keepdims=True))
    soft_b = jnp.exp(scores - log_total).astype(jnp.bfloat16)
    context = jnp.einsum("skgqp,spkd->sqkgd", soft_b, values_b, preferred_element_type=jnp.float32)
    context_b = context.astype(jnp.bfloat16).reshape(row_count, q_width)
    middle = resid_in + matmul(context_b, w_out)
    inv_rms2 = inverse_rms(middle)
    gain2 = gain2_b.astype(jnp.float32)
    normed2 = (middle * inv_rms2 * gain2).astype(jnp.bfloat16)
    back_rows = cotangent.reshape(row_count, model_width)
    normed_all = gather_rows(normed2, pairs)
    gate_pre = matmul(normed_all, gate_weight)
    up_proj = matmul(normed_all, up_weight)
    sigmoid_gate = jax.nn.sigmoid(gate_pre)
    silu_gate = gate_pre * sigmoid_gate
    activ_b = (silu_gate * up_proj).astype(jnp.bfloat16)
    result = middle + scatter_rows(matmul(activ_b, down_weight), pairs)
    back_activ = times_transposed(back_all, down_weight)
    back_gate = (
        back_activ * up_proj * sigmoid_gate * (1.0 + gate_pre * (1.0 - sigmoid_gate))
    ).astype(jnp.bfloat16)
    back_up = (back_activ * silu_gate).astype(jnp.bfloat16)
    grad_down = outer_sum(activ_b, back_all)
    grad_gate = outer_sum(normed_all, back_gate)
    grad_up = outer_sum(normed_all, back_up)
    local_normed = times_transposed(back_gate, gate_weight) + times_transposed(back_up, up_weight)
    back_normed2 = scatter_rows(local_normed, pairs)
    back_norm2, grad_norm2_part = norm_backward(middle, inv_rms2, gain2, back_normed2)
    back_middle = back_rows.astype(jnp.float32) + back_norm2
    back_middle_b = back_middle.astype(jnp.bfloat16)
    grad_out_part = outer_sum(context_b, back_middle_b)
    back_context = times_transposed(back_middle_b, w_out).astype(jnp.bfloat16)
    back_context = back_context.reshape(sequences, length, KV, groups, HD)
    soft = jnp.exp(score_block(query_b, keys_b, allowed, score_scale) - log_total)
    soft_again = soft.astype(jnp.bfloat16)
    back_values = jnp.einsum(
        "skgqp,sqkgd->spkd", soft_again, back_context, preferred_element_type=jnp.float32
    )
    back_soft = jnp.einsum(
        "sqkgd,spkd->skgqp", back_context, values_b, preferred_element_type=jnp.float32
    )
    row_dot = jnp.sum(soft * back_soft, axis=-1, keepdims=True)
    back_scores = (soft * (back_soft - row_dot) * score_scale).astype(jnp.bfloat16)
    back_query = jnp.einsum(
        "skgqp,spkd->sqkgd", back_scores, keys_b, preferred_element_type=jnp.float32
    )
    back_keys = jnp.einsum(
        "skgqp,sqkgd->spkd", back_scores, query_b, preferred_element_type=jnp.float32
    )
    back_query = unrotate(back_query.reshape(sequences, length, H, HD), cosine, sine)
    back_keys = unrotate(back_keys, cosine, sine)
    back_proj = jnp.concatenate(
        [
            back_query.reshape(row_count, q_width),
            back_keys.reshape(row_count, kv_width),
            back_values.reshape(row_count, kv_width),
        ],
        axis=1,
    )
    grad_bias_part = jnp.sum(back_proj, axis=0)
    back_proj_b = back_proj.astype(jnp.bfloat16)
    grad_qkv_part = outer_sum(normed1, back_proj_b)
    back_normed1 = times_transposed(back_proj_b, w_qkv)
    back_norm1, grad_norm1_part = norm_backward(resid_in, inv_rms1, gain1, back_normed1)
    back_tokens = back_middle + back_norm1
    small = jnp.stack([v.reshape(pairs, -1) for v in (grad_norm1_part, grad_norm2_part)], axis=1)
    small = jnp.concatenate(
        [small.reshape(pairs, -1), grad_bias_part.reshape(pairs, -1)], axis=1
    ).reshape(-1)
    owned = sum_owned(
        small,
        grad_qkv_part,
        grad_out_part,
        grad_gate,
        grad_up,
        grad_down,
        pairs,
        copies,
    )
    small, grad_qkv, grad_out, grad_gate, grad_up, grad_down = (
        a.astype(jnp.float32) for a in owned
    )
    gains = norm1_gain.shape[0]
    grad_norm1, grad_norm2, grad_bias = (
        small[:gains],
        small[gains : 2 * gains],
        small[2 * gains :],
    )
    shape_out = (sequences, length, model_width)
    return (
        result.reshape(shape_out),
        back_tokens.reshape(shape_out),
        grad_norm1,
        grad_qkv,
        grad_bias,
        grad_out,
        grad_norm2,
        grad_gate,
        grad_up,
        grad_down,
    )


def solution(mesh):
    in_specs = (
        P(("group", "replica"), None, None),
        P(("group", "replica"), None),
        P("group"),
        P("group", None),
        P("group"),
        P("group", None),
        P("group"),
        P(None, "group"),
        P(None, "group"),
        P("group", None),
        P(("group", "replica"), None, None),
    )
    out_specs = (
        P(("group", "replica"), None, None),
        P(("group", "replica"), None, None),
        P("group"),
        P("group", None),
        P("group"),
        P("group", None),
        P("group"),
        P(None, "group"),
        P(None, "group"),
        P("group", None),
    )
    program = functools.partial(
        on_device, pairs=mesh.shape["group"], copies=mesh.shape["replica"]
    )
    return jax.shard_map(
        program, mesh=mesh, in_specs=in_specs, out_specs=out_specs, check_vma=False
    )
```

```python
import functools

import jax
import jax.numpy as jnp
from jax import lax
from jax.experimental import pallas as pl
from jax.experimental.pallas import tpu as pltpu
from jax.sharding import PartitionSpec as P

H = 14
KV = 2
HD = 64


EPSILON = 1e-06
ROPE_BASE = 1000000.0
NEG_LARGE = -1e30


def doc_layout(segments, head_dim):
    length = segments.shape[1]
    places = jnp.arange(length, dtype=jnp.int32)
    same_doc = segments[:, :, None] == segments[:, None, :]
    earlier = places[None, None, :] < places[None, :, None]
    positions = jnp.sum(jnp.where(same_doc & earlier, 1.0, 0.0).astype(jnp.float32), axis=2)
    allowed = jnp.where(same_doc & (places[None, None, :] <= places[None, :, None]), 1, 0).astype(
        jnp.int32
    )
    half_dim = head_dim // 2
    frequency = ROPE_BASE ** (-2.0 * jnp.arange(half_dim, dtype=jnp.float32) / head_dim)
    angles = positions[:, :, None] * frequency[None, None, :]
    return (allowed, jnp.cos(angles)[:, :, None, :], jnp.sin(angles)[:, :, None, :])


def rotate(values, cosine, sine):
    half_dim = values.shape[-1] // 2
    front_half = values[..., :half_dim]
    back_half = values[..., half_dim:]
    return jnp.concatenate(
        [front_half * cosine - back_half * sine, back_half * cosine + front_half * sine], axis=-1
    )


def unrotate(gradients, cosine, sine):
    half_dim = gradients.shape[-1] // 2
    front_half = gradients[..., :half_dim]
    back_half = gradients[..., half_dim:]
    return jnp.concatenate(
        [front_half * cosine + back_half * sine, back_half * cosine - front_half * sine], axis=-1
    )


def inverse_rms(hidden):
    return lax.rsqrt(jnp.mean(hidden * hidden, axis=-1, keepdims=True) + EPSILON)


def norm_backward(hidden, inv_rms, gain_f, back_normed):
    weighted = back_normed * gain_f
    inner = jnp.mean(weighted * hidden, axis=-1, keepdims=True)
    back_hidden = inv_rms * weighted - hidden * (inv_rms * inv_rms * inv_rms) * inner
    back_gain = jnp.sum(back_normed * hidden * inv_rms, axis=0)
    return (back_hidden, back_gain)


def matmul(left, right):
    return jnp.dot(left, right, preferred_element_type=jnp.float32)


def outer_sum(left, right):
    return lax.dot_general(
        left, right, (((0,), (0,)), ((), ())), preferred_element_type=jnp.float32
    )


def times_transposed(left, right):
    return lax.dot_general(
        left, right, (((1,), (1,)), ((), ())), preferred_element_type=jnp.float32
    )


def score_block(query_b, keys_b, allowed, score_scale):
    scores = (
        jnp.einsum("sqkgd,spkd->skgqp", query_b, keys_b, preferred_element_type=jnp.float32)
        * score_scale
    )
    return jnp.where(allowed[:, None, None, :, :] > 0, scores, NEG_LARGE)


def stage_bits(copies, far_first):
    bits = [1 << i for i in range(copies.bit_length() - 1)]
    if far_first:
        bits = bits[:1] + bits[2:] + bits[1:2]
    return bits


def sum_kernel(copies, pieces, swapped, count, *refs):
    ins, outs = refs[:count], refs[count : 2 * count]
    n = len(pieces)
    held = refs[2 * count : 2 * count + n]
    landed = refs[2 * count + n : 2 * count + 2 * n]
    final = refs[2 * count + 2 * n : 2 * count + 3 * n]
    extra = refs[2 * count + 3 * n : -3]
    send_sem, recv_sem, local_sem = refs[-3:]
    me = lax.axis_index("replica")
    pair = lax.axis_index("group")
    stages = copies.bit_length() - 1
    mesh_id = pl.DeviceIdType.MESH

    def partner(bit):
        return me + bit * (1 - 2 * (lax.div(me, bit) % 2))

    loads = []
    for p, (which, start, width, _, _) in enumerate(pieces):
        source = ins[which].at[pair] if which == swapped else ins[which]
        load = pltpu.make_async_copy(
            source.at[:, :, pl.ds(start, width)], held[p], local_sem.at[p, 0]
        )
        load.start()
        loads.append(load)
    barrier = pltpu.get_barrier_semaphore()
    for i in range(stages):
        pl.semaphore_signal(
            barrier, inc=1, device_id={"replica": partner(1 << i)}, device_id_type=mesh_id
        )
    pl.semaphore_signal(barrier, inc=1, device_id={"group": 1 - pair}, device_id_type=mesh_id)
    pl.semaphore_wait(barrier, stages + 1)

    swaps, at = {}, 0
    for p, (which, start, width, _, _) in enumerate(pieces):
        if which == swapped:
            copy = pltpu.make_async_remote_copy(
                src_ref=ins[which].at[1 - pair].at[:, :, pl.ds(start, width)],
                dst_ref=extra[at],
                send_sem=send_sem.at[p, 2 * stages],
                recv_sem=recv_sem.at[p, 2 * stages],
                device_id={"group": 1 - pair},
                device_id_type=mesh_id,
            )
            copy.start()
            swaps[p] = (copy, extra[at])
            at += 1

    bits = [stage_bits(copies, far) for (_, _, _, far, _) in pieces]
    base = [0] * n
    trail = [[] for _ in range(n)]
    copying = [None] * n
    stores = []

    def accumulate(goal, left, right, first, shift, size):
        def add(i, carry):
            goal[first + i] = left[first + i] + right[shift + i]
            return carry

        lax.fori_loop(0, size, add, 0)

    def spread(p, k):
        block = final[p].at[pl.ds(trail[p][k], copies >> (k + 1))]
        return pltpu.make_async_remote_copy(
            src_ref=block,
            dst_ref=block,
            send_sem=send_sem.at[p, stages + k],
            recv_sem=recv_sem.at[p, stages + k],
            device_id={"replica": partner(bits[p][k])},
            device_id_type=mesh_id,
        )

    def halve(p, k):
        size = copies >> (k + 1)
        bit = bits[p][k]
        side = lax.div(me, bit) % 2
        keep, give = base[p] + side * size, base[p] + (1 - side) * size
        trail[p].append(keep)
        base[p] = keep
        return pltpu.make_async_remote_copy(
            src_ref=held[p].at[pl.ds(give, size)],
            dst_ref=landed[p].at[pl.ds(copies - (copies >> k), size)],
            send_sem=send_sem.at[p, k],
            recv_sem=recv_sem.at[p, k],
            device_id={"replica": partner(bit)},
            device_id_type=mesh_id,
        )

    def step(p, k):
        if k == 0:
            loads[p].wait()
            if p in swaps:
                swaps[p][0].wait()
                accumulate(held[p], held[p], swaps[p][1], 0, 0, copies)
        else:
            copying[p].wait()
            if k <= stages:
                goal = held[p] if k < stages else final[p]
                shift = copies - (copies >> (k - 1))
                accumulate(goal, held[p], landed[p], base[p], shift, copies >> k)
        if k < stages:
            copying[p] = halve(p, k)
        elif k < 2 * stages:
            copying[p] = spread(p, 2 * stages - 1 - k)
        else:
            which, start, width, _, _ = pieces[p]
            store = pltpu.make_async_copy(
                final[p], outs[which].at[:, :, pl.ds(start, width)], local_sem.at[p, 1]
            )
            store.start()
            stores.append(store)
            return
        copying[p].start()

    for tick in range(2 * stages + 1 + max(piece[4] for piece in pieces)):
        for p in range(n):
            k = tick - pieces[p][4]
            if 0 <= k <= 2 * stages:
                step(p, k)
    for store in stores:
        store.wait()


def replica_sum(arrays, copies):
    swapped = len(arrays) - 1
    pieces = []
    for which, array in enumerate(arrays):
        columns = array.shape[-1]
        cut = columns * 4 // 640 * 128
        pieces += [(which, 0, cut, False, which), (which, cut, columns - cut, True, which)]
    stages = copies.bit_length() - 1
    n, count = len(pieces), len(arrays)
    shapes = [(arrays[w].shape[-2], width) for (w, _, width, _, _) in pieces]
    moved = [shape for shape, piece in zip(shapes, pieces) if piece[0] == swapped]
    any_spec = pl.BlockSpec(memory_space=pltpu.HBM)
    return pl.pallas_call(
        functools.partial(sum_kernel, copies, tuple(pieces), swapped, count),
        out_shape=[jax.ShapeDtypeStruct(a.shape[-3:], a.dtype) for a in arrays],
        in_specs=[any_spec] * count,
        out_specs=[any_spec] * count,
        scratch_shapes=[pltpu.VMEM((copies, r, c), jnp.bfloat16) for r, c in shapes]
        + [pltpu.VMEM((copies - 1, r, c), jnp.bfloat16) for r, c in shapes]
        + [pltpu.VMEM((copies, r, c), jnp.bfloat16) for r, c in shapes]
        + [pltpu.VMEM((copies, r, c), jnp.bfloat16) for r, c in moved]
        + [
            pltpu.SemaphoreType.DMA((n, 2 * stages + 1)),
            pltpu.SemaphoreType.DMA((n, 2 * stages + 1)),
            pltpu.SemaphoreType.DMA((n, 2)),
        ],
        compiler_params=pltpu.CompilerParams(
            collective_id=0, has_side_effects=True, vmem_limit_bytes=54 * 1024 * 1024
        ),
        name="replica_sum",
    )(*arrays)


def swap(values):
    return lax.ppermute(values, "group", [(0, 1), (1, 0)])


def gather_weight(shard, pairs, copies):
    if pairs != 2 or copies % 2:
        return lax.all_gather(shard, "group", axis=0, tiled=True)
    half = shard.shape[0] // 2
    core = lax.axis_index("replica") % 2
    mine = swap(lax.dynamic_slice_in_dim(shard, core * half, half, 0))
    sibling = lax.ppermute(mine, "replica", [(i, i + 1 - 2 * (i % 2)) for i in range(copies)])
    front = jnp.where(core == 0, mine, sibling)
    back = jnp.where(core == 0, sibling, mine)
    first = lax.axis_index("group") == 0
    other = jnp.concatenate([front, back], axis=0)
    return jnp.concatenate(
        [jnp.where(first, shard, other), jnp.where(first, other, shard)], axis=0
    )


def gather_vectors(vectors, pairs):
    if pairs != 2:
        return [lax.all_gather(v, "group", axis=0, tiled=True) for v in vectors]
    joined = jnp.concatenate(vectors)
    other = swap(joined)
    first = lax.axis_index("group") == 0
    low, high = jnp.where(first, joined, other), jnp.where(first, other, joined)
    found, at = [], 0
    for v in vectors:
        size = v.shape[0]
        found.append(jnp.concatenate([low[at : at + size], high[at : at + size]]))
        at += size
    return found


def gather_rows(rows, pairs):
    if pairs != 2:
        return lax.all_gather(rows, "group", axis=0, tiled=True)
    return jnp.concatenate([rows, swap(rows)], axis=0)


def scatter_rows(partial, pairs):
    if pairs != 2:
        return lax.psum_scatter(
            partial.astype(jnp.bfloat16), "group", scatter_dimension=0, tiled=True
        ).astype(jnp.float32)
    half = partial.shape[0] // 2
    return partial[:half] + swap(partial[half:].astype(jnp.bfloat16)).astype(jnp.float32)


def scatter_owned(partial):
    return lax.psum_scatter(
        partial.astype(jnp.bfloat16), "group", scatter_dimension=0, tiled=True
    ).astype(jnp.float32)


def sum_owned(small, qkv, out, gate, up, down, pairs, copies):
    rows, width = qkv.shape[0] // pairs, qkv.shape[1] + out.shape[1]
    share = small.shape[0] // pairs
    lines = 64
    fits = (
        copies == 16
        and pairs == 2
        and width % 256 == 0
        and rows + lines == copies // 2 * lines
        and share <= width
        and all(a.shape[0] % (8 * copies) == 0 and a.shape[1] % 128 == 0 for a in (gate, up, down))
    )
    if not fits:
        owned = [scatter_owned(a) for a in (small, qkv, out)]
        return lax.psum(
            tuple(a.astype(jnp.bfloat16) for a in (*owned, gate, up, down)), "replica"
        )
    half = width // 2
    joined = jnp.concatenate([qkv, out], axis=1).astype(jnp.bfloat16)
    joined = jnp.stack([joined[:, :half], joined[:, half:]])
    joined = joined.reshape(2, pairs, rows // lines, lines, half).transpose(1, 0, 2, 3, 4)
    small = small.astype(jnp.bfloat16).reshape(pairs, share)
    line = jnp.pad(small, ((0, 0), (0, width - share))).reshape(pairs, 2, 1, 1, half)
    line = jnp.pad(line, ((0, 0), (0, 0), (0, 0), (0, lines - 1), (0, 0)))
    joined = jnp.concatenate([joined, line], axis=2).reshape(pairs, copies, lines, half)
    folded = [
        a.astype(jnp.bfloat16).reshape(copies, a.shape[0] // copies, a.shape[1])
        for a in (gate, up, down)
    ]
    gate_s, up_s, down_s, joined = replica_sum([*folded, joined], copies)
    joined = joined.reshape(2, rows + lines, half)
    joined = jnp.concatenate([joined[0], joined[1]], axis=1)
    return (
        joined[rows, :share],
        joined[:rows, : qkv.shape[1]],
        joined[:rows, qkv.shape[1] :],
        gate_s.reshape(gate.shape),
        up_s.reshape(up.shape),
        down_s.reshape(down.shape),
    )


def on_device(
    tokens,
    segments,
    norm1_gain,
    qkv_weight,
    qkv_bias,
    out_weight,
    norm2_gain,
    gate_weight,
    up_weight,
    down_weight,
    cotangent,
    *,
    pairs,
    copies,
):
    sequences, length, model_width = tokens.shape
    row_count = sequences * length
    q_width = H * HD
    kv_width = KV * HD
    groups = H // KV
    score_scale = HD ** (-0.5)
    gain1_b, b_qkv, gain2_b = gather_vectors([norm1_gain, qkv_bias, norm2_gain], pairs)
    w_qkv = gather_weight(qkv_weight, pairs, copies)
    back_all = gather_rows(cotangent.reshape(row_count, model_width), pairs)
    w_out = gather_weight(out_weight, pairs, copies)
    allowed, cosine, sine = doc_layout(segments, HD)
    resid_in = tokens.reshape(row_count, model_width).astype(jnp.float32)
    inv_rms1 = inverse_rms(resid_in)
    gain1 = gain1_b.astype(jnp.float32)
    normed1 = (resid_in * inv_rms1 * gain1).astype(jnp.bfloat16)
    projected = matmul(normed1, w_qkv) + b_qkv.astype(jnp.float32)
    query = projected[:, :q_width].reshape(sequences, length, H, HD)
    keys_raw = projected[:, q_width : q_width + kv_width].reshape(sequences, length, KV, HD)
    values_raw = projected[:, q_width + kv_width :].reshape(sequences, length, KV, HD)
    query_b = (
        rotate(query, cosine, sine).astype(jnp.bfloat16).reshape(sequences, length, KV, groups, HD)
    )
    keys_b = rotate(keys_raw, cosine, sine).astype(jnp.bfloat16)
    values_b = values_raw.astype(jnp.bfloat16)
    scores = score_block(query_b, keys_b, allowed, score_scale)
    top_score = jnp.max(scores, axis=-1, keepdims=True)
    log_total = top_score + jnp.log(jnp.sum(jnp.exp(scores - top_score), axis=-1, keepdims=True))
    soft_b = jnp.exp(scores - log_total).astype(jnp.bfloat16)
    context = jnp.einsum("skgqp,spkd->sqkgd", soft_b, values_b, preferred_element_type=jnp.float32)
    context_b = context.astype(jnp.bfloat16).reshape(row_count, q_width)
    middle = resid_in + matmul(context_b, w_out)
    inv_rms2 = inverse_rms(middle)
    gain2 = gain2_b.astype(jnp.float32)
    normed2 = (middle * inv_rms2 * gain2).astype(jnp.bfloat16)
    back_rows = cotangent.reshape(row_count, model_width)
    normed_all = gather_rows(normed2, pairs)
    gate_pre = matmul(normed_all, gate_weight)
    up_proj = matmul(normed_all, up_weight)
    sigmoid_gate = jax.nn.sigmoid(gate_pre)
    silu_gate = gate_pre * sigmoid_gate
    activ_b = (silu_gate * up_proj).astype(jnp.bfloat16)
    result = middle + scatter_rows(matmul(activ_b, down_weight), pairs)
    back_activ = times_transposed(back_all, down_weight)
    back_gate = (
        back_activ * up_proj * sigmoid_gate * (1.0 + gate_pre * (1.0 - sigmoid_gate))
    ).astype(jnp.bfloat16)
    back_up = (back_activ * silu_gate).astype(jnp.bfloat16)
    grad_down = outer_sum(activ_b, back_all)
    grad_gate = outer_sum(normed_all, back_gate)
    grad_up = outer_sum(normed_all, back_up)
    local_normed = times_transposed(back_gate, gate_weight) + times_transposed(back_up, up_weight)
    back_normed2 = scatter_rows(local_normed, pairs)
    back_norm2, grad_norm2_part = norm_backward(middle, inv_rms2, gain2, back_normed2)
    back_middle = back_rows.astype(jnp.float32) + back_norm2
    back_middle_b = back_middle.astype(jnp.bfloat16)
    grad_out_part = outer_sum(context_b, back_middle_b)
    back_context = times_transposed(back_middle_b, w_out).astype(jnp.bfloat16)
    back_context = back_context.reshape(sequences, length, KV, groups, HD)
    soft = jnp.exp(score_block(query_b, keys_b, allowed, score_scale) - log_total)
    soft_again = soft.astype(jnp.bfloat16)
    back_values = jnp.einsum(
        "skgqp,sqkgd->spkd", soft_again, back_context, preferred_element_type=jnp.float32
    )
    back_soft = jnp.einsum(
        "sqkgd,spkd->skgqp", back_context, values_b, preferred_element_type=jnp.float32
    )
    row_dot = jnp.sum(soft * back_soft, axis=-1, keepdims=True)
    back_scores = (soft * (back_soft - row_dot) * score_scale).astype(jnp.bfloat16)
    back_query = jnp.einsum(
        "skgqp,spkd->sqkgd", back_scores, keys_b, preferred_element_type=jnp.float32
    )
    back_keys = jnp.einsum(
        "skgqp,sqkgd->spkd", back_scores, query_b, preferred_element_type=jnp.float32
    )
    back_query = unrotate(back_query.reshape(sequences, length, H, HD), cosine, sine)
    back_keys = unrotate(back_keys, cosine, sine)
    back_proj = jnp.concatenate(
        [
            back_query.reshape(row_count, q_width),
            back_keys.reshape(row_count, kv_width),
            back_values.reshape(row_count, kv_width),
        ],
        axis=1,
    )
    grad_bias_part = jnp.sum(back_proj, axis=0)
    back_proj_b = back_proj.astype(jnp.bfloat16)
    grad_qkv_part = outer_sum(normed1, back_proj_b)
    back_normed1 = times_transposed(back_proj_b, w_qkv)
    back_norm1, grad_norm1_part = norm_backward(resid_in, inv_rms1, gain1, back_normed1)
    back_tokens = back_middle + back_norm1
    small = jnp.stack([v.reshape(pairs, -1) for v in (grad_norm1_part, grad_norm2_part)], axis=1)
    small = jnp.concatenate(
        [small.reshape(pairs, -1), grad_bias_part.reshape(pairs, -1)], axis=1
    ).reshape(-1)
    owned = sum_owned(
        small,
        grad_qkv_part,
        grad_out_part,
        grad_gate,
        grad_up,
        grad_down,
        pairs,
        copies,
    )
    small, grad_qkv, grad_out, grad_gate, grad_up, grad_down = (
        a.astype(jnp.float32) for a in owned
    )
    gains = norm1_gain.shape[0]
    grad_norm1, grad_norm2, grad_bias = (
        small[:gains],
        small[gains : 2 * gains],
        small[2 * gains :],
    )
    shape_out = (sequences, length, model_width)
    return (
        result.reshape(shape_out),
        back_tokens.reshape(shape_out),
        grad_norm1,
        grad_qkv,
        grad_bias,
        grad_out,
        grad_norm2,
        grad_gate,
        grad_up,
        grad_down,
    )


def solution(mesh):
    in_specs = (
        P(("group", "replica"), None, None),
        P(("group", "replica"), None),
        P("group"),
        P("group", None),
        P("group"),
        P("group", None),
        P("group"),
        P(None, "group"),
        P(None, "group"),
        P("group", None),
        P(("group", "replica"), None, None),
    )
    out_specs = (
        P(("group", "replica"), None, None),
        P(("group", "replica"), None, None),
        P("group"),
        P("group", None),
        P("group"),
        P("group", None),
        P("group"),
        P(None, "group"),
        P(None, "group"),
        P("group", None),
    )
    program = functools.partial(
        on_device, pairs=mesh.shape["group"], copies=mesh.shape["replica"]
    )
    return jax.shard_map(
        program, mesh=mesh, in_specs=in_specs, out_specs=out_specs, check_vma=False
    )
```

```python
import functools

import jax
import jax.numpy as jnp
from jax import lax
from jax.experimental import pallas as pl
from jax.experimental.pallas import tpu as pltpu
from jax.sharding import PartitionSpec as P

H = 14
KV = 2
HD = 64


EPSILON = 1e-06
ROPE_BASE = 1000000.0
NEG_LARGE = -1e30


def doc_layout(segments, head_dim):
    length = segments.shape[1]
    places = jnp.arange(length, dtype=jnp.int32)
    same_doc = segments[:, :, None] == segments[:, None, :]
    earlier = places[None, None, :] < places[None, :, None]
    positions = jnp.sum(jnp.where(same_doc & earlier, 1.0, 0.0).astype(jnp.float32), axis=2)
    allowed = jnp.where(same_doc & (places[None, None, :] <= places[None, :, None]), 1, 0).astype(
        jnp.int32
    )
    half_dim = head_dim // 2
    frequency = ROPE_BASE ** (-2.0 * jnp.arange(half_dim, dtype=jnp.float32) / head_dim)
    angles = positions[:, :, None] * frequency[None, None, :]
    return (allowed, jnp.cos(angles)[:, :, None, :], jnp.sin(angles)[:, :, None, :])


def rotate(values, cosine, sine):
    half_dim = values.shape[-1] // 2
    front_half = values[..., :half_dim]
    back_half = values[..., half_dim:]
    return jnp.concatenate(
        [front_half * cosine - back_half * sine, back_half * cosine + front_half * sine], axis=-1
    )


def unrotate(gradients, cosine, sine):
    half_dim = gradients.shape[-1] // 2
    front_half = gradients[..., :half_dim]
    back_half = gradients[..., half_dim:]
    return jnp.concatenate(
        [front_half * cosine + back_half * sine, back_half * cosine - front_half * sine], axis=-1
    )


def inverse_rms(hidden):
    return lax.rsqrt(jnp.mean(hidden * hidden, axis=-1, keepdims=True) + EPSILON)


def norm_backward(hidden, inv_rms, gain_f, back_normed):
    weighted = back_normed * gain_f
    inner = jnp.mean(weighted * hidden, axis=-1, keepdims=True)
    back_hidden = inv_rms * weighted - hidden * (inv_rms * inv_rms * inv_rms) * inner
    back_gain = jnp.sum(back_normed * hidden * inv_rms, axis=0)
    return (back_hidden, back_gain)


def matmul(left, right):
    return jnp.dot(left, right, preferred_element_type=jnp.float32)


def outer_sum(left, right):
    return lax.dot_general(
        left, right, (((0,), (0,)), ((), ())), preferred_element_type=jnp.float32
    )


def times_transposed(left, right):
    return lax.dot_general(
        left, right, (((1,), (1,)), ((), ())), preferred_element_type=jnp.float32
    )


def score_block(query_b, keys_b, allowed, score_scale):
    scores = (
        jnp.einsum("sqkgd,spkd->skgqp", query_b, keys_b, preferred_element_type=jnp.float32)
        * score_scale
    )
    return jnp.where(allowed[:, None, None, :, :] > 0, scores, NEG_LARGE)


def stage_bits(copies, far_first):
    bits = [1 << i for i in range(copies.bit_length() - 1)]
    if far_first:
        bits = bits[:1] + bits[2:] + bits[1:2]
    return bits


def sum_kernel(copies, pieces, swapped, count, *refs):
    ins, outs = refs[:count], refs[count : 2 * count]
    n = len(pieces)
    held = refs[2 * count : 2 * count + n]
    landed = refs[2 * count + n : 2 * count + 2 * n]
    final = refs[2 * count + 2 * n : 2 * count + 3 * n]
    extra = refs[2 * count + 3 * n : -3]
    send_sem, recv_sem, local_sem = refs[-3:]
    me = lax.axis_index("replica")
    pair = lax.axis_index("group")
    stages = copies.bit_length() - 1
    mesh_id = pl.DeviceIdType.MESH

    def partner(bit):
        return me + bit * (1 - 2 * (lax.div(me, bit) % 2))

    loads = []
    for p, (which, start, width, _, _) in enumerate(pieces):
        source = ins[which].at[pair] if which == swapped else ins[which]
        load = pltpu.make_async_copy(
            source.at[:, :, pl.ds(start, width)], held[p], local_sem.at[p, 0]
        )
        load.start()
        loads.append(load)
    barrier = pltpu.get_barrier_semaphore()
    for i in range(stages):
        pl.semaphore_signal(
            barrier, inc=1, device_id={"replica": partner(1 << i)}, device_id_type=mesh_id
        )
    pl.semaphore_signal(barrier, inc=1, device_id={"group": 1 - pair}, device_id_type=mesh_id)
    pl.semaphore_wait(barrier, stages + 1)

    swaps, at = {}, 0
    for p, (which, start, width, _, _) in enumerate(pieces):
        if which == swapped:
            copy = pltpu.make_async_remote_copy(
                src_ref=ins[which].at[1 - pair].at[:, :, pl.ds(start, width)],
                dst_ref=extra[at],
                send_sem=send_sem.at[p, 2 * stages],
                recv_sem=recv_sem.at[p, 2 * stages],
                device_id={"group": 1 - pair},
                device_id_type=mesh_id,
            )
            copy.start()
            swaps[p] = (copy, extra[at])
            at += 1

    bits = [stage_bits(copies, far) for (_, _, _, far, _) in pieces]
    base = [0] * n
    trail = [[] for _ in range(n)]
    copying = [None] * n
    stores = []

    def accumulate(goal, left, right, first, shift, size):
        def add(i, carry):
            goal[first + i] = left[first + i] + right[shift + i]
            return carry

        lax.fori_loop(0, size, add, 0)

    def spread(p, k):
        block = final[p].at[pl.ds(trail[p][k], copies >> (k + 1))]
        return pltpu.make_async_remote_copy(
            src_ref=block,
            dst_ref=block,
            send_sem=send_sem.at[p, stages + k],
            recv_sem=recv_sem.at[p, stages + k],
            device_id={"replica": partner(bits[p][k])},
            device_id_type=mesh_id,
        )

    def halve(p, k):
        size = copies >> (k + 1)
        bit = bits[p][k]
        side = lax.div(me, bit) % 2
        keep, give = base[p] + side * size, base[p] + (1 - side) * size
        trail[p].append(keep)
        base[p] = keep
        return pltpu.make_async_remote_copy(
            src_ref=held[p].at[pl.ds(give, size)],
            dst_ref=landed[p].at[pl.ds(copies - (copies >> k), size)],
            send_sem=send_sem.at[p, k],
            recv_sem=recv_sem.at[p, k],
            device_id={"replica": partner(bit)},
            device_id_type=mesh_id,
        )

    def step(p, k):
        if k == 0:
            loads[p].wait()
            if p in swaps:
                swaps[p][0].wait()
                accumulate(held[p], held[p], swaps[p][1], 0, 0, copies)
        else:
            copying[p].wait()
            if k <= stages:
                goal = held[p] if k < stages else final[p]
                shift = copies - (copies >> (k - 1))
                accumulate(goal, held[p], landed[p], base[p], shift, copies >> k)
        if k < stages:
            copying[p] = halve(p, k)
        elif k < 2 * stages:
            copying[p] = spread(p, 2 * stages - 1 - k)
        else:
            which, start, width, _, _ = pieces[p]
            store = pltpu.make_async_copy(
                final[p], outs[which].at[:, :, pl.ds(start, width)], local_sem.at[p, 1]
            )
            store.start()
            stores.append(store)
            return
        copying[p].start()

    for tick in range(2 * stages + 1 + max(piece[4] for piece in pieces)):
        for p in range(n):
            k = tick - pieces[p][4]
            if 0 <= k <= 2 * stages:
                step(p, k)
    for store in stores:
        store.wait()


def replica_sum(arrays, copies):
    swapped = len(arrays) - 1
    pieces = []
    for which, array in enumerate(arrays):
        columns = array.shape[-1]
        cut = columns * 4 // 640 * 128
        pieces += [(which, 0, cut, False, which), (which, cut, columns - cut, True, which)]
    stages = copies.bit_length() - 1
    n, count = len(pieces), len(arrays)
    shapes = [(arrays[w].shape[-2], width) for (w, _, width, _, _) in pieces]
    moved = [shape for shape, piece in zip(shapes, pieces) if piece[0] == swapped]
    any_spec = pl.BlockSpec(memory_space=pltpu.HBM)
    return pl.pallas_call(
        functools.partial(sum_kernel, copies, tuple(pieces), swapped, count),
        out_shape=[jax.ShapeDtypeStruct(a.shape[-3:], a.dtype) for a in arrays],
        in_specs=[any_spec] * count,
        out_specs=[any_spec] * count,
        scratch_shapes=[pltpu.VMEM((copies, r, c), jnp.bfloat16) for r, c in shapes]
        + [pltpu.VMEM((copies - 1, r, c), jnp.bfloat16) for r, c in shapes]
        + [pltpu.VMEM((copies, r, c), jnp.bfloat16) for r, c in shapes]
        + [pltpu.VMEM((copies, r, c), jnp.bfloat16) for r, c in moved]
        + [
            pltpu.SemaphoreType.DMA((n, 2 * stages + 1)),
            pltpu.SemaphoreType.DMA((n, 2 * stages + 1)),
            pltpu.SemaphoreType.DMA((n, 2)),
        ],
        compiler_params=pltpu.CompilerParams(
            collective_id=0, has_side_effects=True, vmem_limit_bytes=54 * 1024 * 1024
        ),
        cost_estimate=pl.CostEstimate(
            flops=0, bytes_accessed=200 * 1024 * 1024, transcendentals=0
        ),
        name="replica_sum",
    )(*arrays)


def swap(values):
    return lax.ppermute(values, "group", [(0, 1), (1, 0)])


def gather_weight(shard, pairs, copies):
    if pairs != 2 or copies % 2:
        return lax.all_gather(shard, "group", axis=0, tiled=True)
    half = shard.shape[0] // 2
    core = lax.axis_index("replica") % 2
    mine = swap(lax.dynamic_slice_in_dim(shard, core * half, half, 0))
    sibling = lax.ppermute(mine, "replica", [(i, i + 1 - 2 * (i % 2)) for i in range(copies)])
    front = jnp.where(core == 0, mine, sibling)
    back = jnp.where(core == 0, sibling, mine)
    first = lax.axis_index("group") == 0
    other = jnp.concatenate([front, back], axis=0)
    return jnp.concatenate(
        [jnp.where(first, shard, other), jnp.where(first, other, shard)], axis=0
    )


def gather_vectors(vectors, pairs):
    if pairs != 2:
        return [lax.all_gather(v, "group", axis=0, tiled=True) for v in vectors]
    joined = jnp.concatenate(vectors)
    other = swap(joined)
    first = lax.axis_index("group") == 0
    low, high = jnp.where(first, joined, other), jnp.where(first, other, joined)
    found, at = [], 0
    for v in vectors:
        size = v.shape[0]
        found.append(jnp.concatenate([low[at : at + size], high[at : at + size]]))
        at += size
    return found


def gather_rows(rows, pairs):
    if pairs != 2:
        return lax.all_gather(rows, "group", axis=0, tiled=True)
    return jnp.concatenate([rows, swap(rows)], axis=0)


def scatter_rows(partial, pairs):
    if pairs != 2:
        return lax.psum_scatter(
            partial.astype(jnp.bfloat16), "group", scatter_dimension=0, tiled=True
        ).astype(jnp.float32)
    half = partial.shape[0] // 2
    return partial[:half] + swap(partial[half:].astype(jnp.bfloat16)).astype(jnp.float32)


def scatter_owned(partial):
    return lax.psum_scatter(
        partial.astype(jnp.bfloat16), "group", scatter_dimension=0, tiled=True
    ).astype(jnp.float32)


def sum_owned(small, qkv, out, gate, up, down, pairs, copies):
    rows, width = qkv.shape[0] // pairs, qkv.shape[1] + out.shape[1]
    share = small.shape[0] // pairs
    lines = 64
    fits = (
        copies == 16
        and pairs == 2
        and width % 256 == 0
        and rows + lines == copies // 2 * lines
        and share <= width
        and all(a.shape[0] % (8 * copies) == 0 and a.shape[1] % 128 == 0 for a in (gate, up, down))
    )
    if not fits:
        owned = [scatter_owned(a) for a in (small, qkv, out)]
        return lax.psum(
            tuple(a.astype(jnp.bfloat16) for a in (*owned, gate, up, down)), "replica"
        )
    half = width // 2
    joined = jnp.concatenate([qkv, out], axis=1).astype(jnp.bfloat16)
    joined = jnp.stack([joined[:, :half], joined[:, half:]])
    joined = joined.reshape(2, pairs, rows // lines, lines, half).transpose(1, 0, 2, 3, 4)
    small = small.astype(jnp.bfloat16).reshape(pairs, share)
    line = jnp.pad(small, ((0, 0), (0, width - share))).reshape(pairs, 2, 1, 1, half)
    line = jnp.pad(line, ((0, 0), (0, 0), (0, 0), (0, lines - 1), (0, 0)))
    joined = jnp.concatenate([joined, line], axis=2).reshape(pairs, copies, lines, half)
    folded = [
        a.astype(jnp.bfloat16).reshape(copies, a.shape[0] // copies, a.shape[1])
        for a in (up, down)
    ]
    gate_s = lax.psum(gate.astype(jnp.bfloat16), "replica")
    up_s, down_s, joined = replica_sum([*folded, joined], copies)
    joined = joined.reshape(2, rows + lines, half)
    joined = jnp.concatenate([joined[0], joined[1]], axis=1)
    return (
        joined[rows, :share],
        joined[:rows, : qkv.shape[1]],
        joined[:rows, qkv.shape[1] :],
        gate_s,
        up_s.reshape(up.shape),
        down_s.reshape(down.shape),
    )


def on_device(
    tokens,
    segments,
    norm1_gain,
    qkv_weight,
    qkv_bias,
    out_weight,
    norm2_gain,
    gate_weight,
    up_weight,
    down_weight,
    cotangent,
    *,
    pairs,
    copies,
):
    sequences, length, model_width = tokens.shape
    row_count = sequences * length
    q_width = H * HD
    kv_width = KV * HD
    groups = H // KV
    score_scale = HD ** (-0.5)
    gain1_b, b_qkv, gain2_b = gather_vectors([norm1_gain, qkv_bias, norm2_gain], pairs)
    w_qkv = gather_weight(qkv_weight, pairs, copies)
    back_all = gather_rows(cotangent.reshape(row_count, model_width), pairs)
    w_out = gather_weight(out_weight, pairs, copies)
    allowed, cosine, sine = doc_layout(segments, HD)
    resid_in = tokens.reshape(row_count, model_width).astype(jnp.float32)
    inv_rms1 = inverse_rms(resid_in)
    gain1 = gain1_b.astype(jnp.float32)
    normed1 = (resid_in * inv_rms1 * gain1).astype(jnp.bfloat16)
    projected = matmul(normed1, w_qkv) + b_qkv.astype(jnp.float32)
    query = projected[:, :q_width].reshape(sequences, length, H, HD)
    keys_raw = projected[:, q_width : q_width + kv_width].reshape(sequences, length, KV, HD)
    values_raw = projected[:, q_width + kv_width :].reshape(sequences, length, KV, HD)
    query_b = (
        rotate(query, cosine, sine).astype(jnp.bfloat16).reshape(sequences, length, KV, groups, HD)
    )
    keys_b = rotate(keys_raw, cosine, sine).astype(jnp.bfloat16)
    values_b = values_raw.astype(jnp.bfloat16)
    scores = score_block(query_b, keys_b, allowed, score_scale)
    top_score = jnp.max(scores, axis=-1, keepdims=True)
    log_total = top_score + jnp.log(jnp.sum(jnp.exp(scores - top_score), axis=-1, keepdims=True))
    soft_b = jnp.exp(scores - log_total).astype(jnp.bfloat16)
    context = jnp.einsum("skgqp,spkd->sqkgd", soft_b, values_b, preferred_element_type=jnp.float32)
    context_b = context.astype(jnp.bfloat16).reshape(row_count, q_width)
    middle = resid_in + matmul(context_b, w_out)
    inv_rms2 = inverse_rms(middle)
    gain2 = gain2_b.astype(jnp.float32)
    normed2 = (middle * inv_rms2 * gain2).astype(jnp.bfloat16)
    back_rows = cotangent.reshape(row_count, model_width)
    normed_all = gather_rows(normed2, pairs)
    gate_pre = matmul(normed_all, gate_weight)
    up_proj = matmul(normed_all, up_weight)
    sigmoid_gate = jax.nn.sigmoid(gate_pre)
    silu_gate = gate_pre * sigmoid_gate
    activ_b = (silu_gate * up_proj).astype(jnp.bfloat16)
    result = middle + scatter_rows(matmul(activ_b, down_weight), pairs)
    back_activ = times_transposed(back_all, down_weight)
    back_gate = (
        back_activ * up_proj * sigmoid_gate * (1.0 + gate_pre * (1.0 - sigmoid_gate))
    ).astype(jnp.bfloat16)
    back_up = (back_activ * silu_gate).astype(jnp.bfloat16)
    grad_down = outer_sum(activ_b, back_all)
    grad_gate = outer_sum(normed_all, back_gate)
    grad_up = outer_sum(normed_all, back_up)
    local_normed = times_transposed(back_gate, gate_weight) + times_transposed(back_up, up_weight)
    back_normed2 = scatter_rows(local_normed, pairs)
    back_norm2, grad_norm2_part = norm_backward(middle, inv_rms2, gain2, back_normed2)
    back_middle = back_rows.astype(jnp.float32) + back_norm2
    back_middle_b = back_middle.astype(jnp.bfloat16)
    grad_out_part = outer_sum(context_b, back_middle_b)
    back_context = times_transposed(back_middle_b, w_out).astype(jnp.bfloat16)
    back_context = back_context.reshape(sequences, length, KV, groups, HD)
    soft = jnp.exp(score_block(query_b, keys_b, allowed, score_scale) - log_total)
    soft_again = soft.astype(jnp.bfloat16)
    back_values = jnp.einsum(
        "skgqp,sqkgd->spkd", soft_again, back_context, preferred_element_type=jnp.float32
    )
    back_soft = jnp.einsum(
        "sqkgd,spkd->skgqp", back_context, values_b, preferred_element_type=jnp.float32
    )
    row_dot = jnp.sum(soft * back_soft, axis=-1, keepdims=True)
    back_scores = (soft * (back_soft - row_dot) * score_scale).astype(jnp.bfloat16)
    back_query = jnp.einsum(
        "skgqp,spkd->sqkgd", back_scores, keys_b, preferred_element_type=jnp.float32
    )
    back_keys = jnp.einsum(
        "skgqp,sqkgd->spkd", back_scores, query_b, preferred_element_type=jnp.float32
    )
    back_query = unrotate(back_query.reshape(sequences, length, H, HD), cosine, sine)
    back_keys = unrotate(back_keys, cosine, sine)
    back_proj = jnp.concatenate(
        [
            back_query.reshape(row_count, q_width),
            back_keys.reshape(row_count, kv_width),
            back_values.reshape(row_count, kv_width),
        ],
        axis=1,
    )
    grad_bias_part = jnp.sum(back_proj, axis=0)
    back_proj_b = back_proj.astype(jnp.bfloat16)
    grad_qkv_part = outer_sum(normed1, back_proj_b)
    back_normed1 = times_transposed(back_proj_b, w_qkv)
    back_norm1, grad_norm1_part = norm_backward(resid_in, inv_rms1, gain1, back_normed1)
    back_tokens = back_middle + back_norm1
    small = jnp.stack([v.reshape(pairs, -1) for v in (grad_norm1_part, grad_norm2_part)], axis=1)
    small = jnp.concatenate(
        [small.reshape(pairs, -1), grad_bias_part.reshape(pairs, -1)], axis=1
    ).reshape(-1)
    owned = sum_owned(
        small,
        grad_qkv_part,
        grad_out_part,
        grad_gate,
        grad_up,
        grad_down,
        pairs,
        copies,
    )
    small, grad_qkv, grad_out, grad_gate, grad_up, grad_down = (
        a.astype(jnp.float32) for a in owned
    )
    gains = norm1_gain.shape[0]
    grad_norm1, grad_norm2, grad_bias = (
        small[:gains],
        small[gains : 2 * gains],
        small[2 * gains :],
    )
    shape_out = (sequences, length, model_width)
    return (
        result.reshape(shape_out),
        back_tokens.reshape(shape_out),
        grad_norm1,
        grad_qkv,
        grad_bias,
        grad_out,
        grad_norm2,
        grad_gate,
        grad_up,
        grad_down,
    )


def solution(mesh):
    in_specs = (
        P(("group", "replica"), None, None),
        P(("group", "replica"), None),
        P("group"),
        P("group", None),
        P("group"),
        P("group", None),
        P("group"),
        P(None, "group"),
        P(None, "group"),
        P("group", None),
        P(("group", "replica"), None, None),
    )
    out_specs = (
        P(("group", "replica"), None, None),
        P(("group", "replica"), None, None),
        P("group"),
        P("group", None),
        P("group"),
        P("group", None),
        P("group"),
        P(None, "group"),
        P(None, "group"),
        P("group", None),
    )
    program = functools.partial(
        on_device, pairs=mesh.shape["group"], copies=mesh.shape["replica"]
    )
    return jax.shard_map(
        program, mesh=mesh, in_specs=in_specs, out_specs=out_specs, check_vma=False
    )
```
